32 devices in a mesh: mem: 4 (over y, x), gx: 4 (over z), gy: 2 (over core).
Axes of the slice: x: 2, y: 2, z: 4, core: 2. Of those that a mesh axis runs over, the one named last changes fastest.
Arguments:
- control: float32 [2, 16, 512, 512], P(None, 'mem', 'gx', 'gy'), may hold values from -6 to 6
- members: float32 [8, 2, 16, 256, 256], P('mem', None, None, 'gx', 'gy'), may hold values from -6 to 6
- diffusivity: float32 [16, 256, 256], P(None, 'gx', 'gy'), may hold values from 0.05 to 0.4
- rotation: float32 [256, 256], P('gx', 'gy'), may hold values from -1 to 1
Outputs:
- control_final: float32 [2, 16, 512, 512], P(None, 'mem', 'gx', 'gy')
- members_final: float32 [8, 2, 16, 256, 256], P('mem', None, None, 'gx', 'gy')
The draws below stay inside these ranges and needn't reach their ends.
All inputs are finite; a program needn't handle non-finite values.
Results may differ from the reference program's by a relative error of at most 0.00002.
Values sent between devices are 32-bit elements; how exact they have to be, the bound alone decides.
A program may use at most 128 MiB of HBM per device.

```python
import math
import jax
import jax.numpy as jnp
from jax import lax

LEV = 16
CSTEPS = 4
MSTEPS = 4
NX = 512
NY = 512
MX = 256
MY = 256
MEMBERS = 8


def level_of(stream_key, dims, pieces, low, largest):
    factor_of = 1.0
    for axis_at, parts in pieces:
        heights = jax.random.uniform(jax.random.fold_in(jax.random.fold_in(stream_key, 6), axis_at), (parts,), jnp.float32, low / len(pieces), largest / len(pieces))
        factor_of = factor_of * jnp.repeat(jnp.exp(heights), dims[axis_at] // parts).reshape((-1,) + (1,) * (len(dims) - 1 - axis_at))
    return factor_of


def gaussian(stream_key, extent, deviation, bound, pieces=(), dtype=jnp.bfloat16):
    values = jax.random.normal(stream_key, extent, jnp.float32) * deviation
    if len(pieces) > 0:
        values = level_of(stream_key, extent, pieces, -0.22, 0.18) * values
    return jnp.clip(values, min=-bound, max=bound).astype(dtype)


def setup_inputs(seed: int = 0) -> dict:
    streams_of = jax.random.split(jax.random.key(seed), 5)
    control = gaussian(streams_of[0], (2, LEV, NX, NY), 1.0, 6.0, ((1, 4), (2, 4), (3, 2)), jnp.float32)
    members = gaussian(streams_of[1], (MEMBERS, 2, LEV, MX, MY), 1.0, 6.0, ((0, 4), (3, 4), (4, 2)), jnp.float32)
    diffusivity = jnp.clip(jnp.exp(math.log(0.4) - 2.0794415 * jax.random.uniform(streams_of[2], (LEV, MX, MY), jnp.float32) ** level_of(streams_of[2], (LEV, MX, MY), ((1, 4), (2, 2)), -0.2, 0.2)), 0.05, 0.4)
    rotation = jnp.clip(jax.random.uniform(streams_of[3], (MX, MY), jnp.float32, -1.0, 1.0) * level_of(streams_of[3], (MX, MY), ((0, 4), (1, 2)), -0.4, 0.0), -1.0, 1.0)
    return {"control": control, "members": members, "diffusivity": diffusivity, "rotation": rotation}


step_control = 0.15
viscosity = 0.5
step_member = 0.5


def control_step(fields):
    upper_x = jnp.roll(fields, -1, axis=-2)
    lower_x = jnp.roll(fields, 1, axis=-2)
    upper_y = jnp.roll(fields, -1, axis=-1)
    lower_y = jnp.roll(fields, 1, axis=-1)
    along_x = (upper_x - lower_x) * 0.5
    along_y = (upper_y - lower_y) * 0.5
    laplace = upper_x + lower_x + upper_y + lower_y - 4.0 * fields
    speed_x = fields[0:1]
    speed_y = fields[1:2]
    return fields + step_control * (-speed_x * along_x - speed_y * along_y + viscosity * laplace)


def member_step(ensemble, east, west, north, south, rotation):
    upper_x = jnp.roll(ensemble, -1, axis=-2)
    lower_x = jnp.roll(ensemble, 1, axis=-2)
    upper_y = jnp.roll(ensemble, -1, axis=-1)
    lower_y = jnp.roll(ensemble, 1, axis=-1)
    spread = east * (upper_x - ensemble) - west * (ensemble - lower_x) + north * (upper_y - ensemble) - south * (ensemble - lower_y)
    first = ensemble[:, 0]
    second = ensemble[:, 1]
    new_first = first + step_member * (spread[:, 0] - rotation * second)
    new_second = second + step_member * (spread[:, 1] + rotation * first)
    return jnp.stack([new_first, new_second], axis=1)


def reference(control, members, diffusivity, rotation):
    def per_level(inputs):
        fields, ensemble, kappa = inputs
        for repeat in range(CSTEPS):
            fields = control_step(fields)
        restricted = fields.reshape(2, NX // 2, 2, NY // 2, 2).sum(axis=(2, 4)) * 0.25
        mean = jnp.sum(ensemble, axis=0) / MEMBERS
        ensemble = ensemble + (restricted - mean)[None]
        east = 0.5 * (kappa + jnp.roll(kappa, -1, axis=-2))
        west = 0.5 * (jnp.roll(kappa, 1, axis=-2) + kappa)
        north = 0.5 * (kappa + jnp.roll(kappa, -1, axis=-1))
        south = 0.5 * (jnp.roll(kappa, 1, axis=-1) + kappa)
        for repeat in range(MSTEPS):
            ensemble = member_step(ensemble, east, west, north, south, rotation)
        return fields, ensemble

    control_levels = jnp.moveaxis(control, 1, 0)
    member_levels = jnp.moveaxis(members, 2, 0)
    fields_out, ensemble_out = lax.map(per_level, (control_levels, member_levels, diffusivity))
    return jnp.moveaxis(fields_out, 0, 1), jnp.moveaxis(ensemble_out, 0, 2)
```

```python
import functools

import jax
import jax.numpy as jnp
from jax import lax
from jax.experimental import pallas as pl
from jax.experimental.pallas import tpu as pltpu
from jax.sharding import PartitionSpec as P

CSTEPS = 4
MSTEPS = 4
H = 4
SLOT = 2 * H
LANES = 128

step_control = 0.15
viscosity = 0.5
step_member = 0.5
F32 = jnp.float32


def cost(flops, size):
    return pl.CostEstimate(flops=flops, bytes_accessed=size, transcendentals=0)


def whole(shape):
    return pl.BlockSpec(shape, lambda *_: (0,) * len(shape))


def lane_ids(rows):
    return lax.broadcasted_iota(jnp.int32, (rows, LANES), 1)


def put_slot(packed, edges, slot):
    shift = H + SLOT * slot
    if not isinstance(slot, int):
        shift = lax.rem(shift, LANES)
    rolled = pltpu.roll(edges, shift, 1)
    ids = lane_ids(edges.shape[0])
    inside = (ids >= SLOT * slot) & (ids < SLOT * slot + SLOT)
    return jnp.where(inside, rolled, packed)


def side_block(left, right, slot):
    shift = lax.rem(2 * LANES - SLOT * slot - H, LANES)
    after = pltpu.roll(right, shift, 1)
    if left is right:
        return after
    before = pltpu.roll(left, shift, 1)
    return jnp.where(lane_ids(after.shape[0]) < LANES // 2, after, before)


def pack_kernel(c_ref, m_ref, d_ref, r_ref, pc_ref, pm_ref, sum_ref, hm_ref, tm_ref, hc_ref, tc_ref):
    fields, clevels, crows, ccols = c_ref.shape
    count, mf, levels, rows, cols = m_ref.shape
    ids = lane_ids(crows)
    packed = jnp.zeros((crows, LANES), F32)
    for f in range(fields):
        for l in range(clevels):
            first = c_ref[f, l, :, :LANES]
            last = c_ref[f, l, :, ccols - LANES :]
            edges = jnp.where(ids < LANES // 2, first, last)
            packed = put_slot(packed, edges, f * clevels + l)
            hc_ref[f, l] = c_ref[f, l, :H]
            tc_ref[f, l] = c_ref[f, l, crows - H :]
    pc_ref[0] = packed

    def edges_of(tile, at):
        hm_ref[at] = tile[:H]
        tm_ref[at] = tile[rows - H :]

    for f in range(mf):
        packs = [jnp.zeros((rows, LANES), F32) for _ in range(count)]
        for l in range(levels):
            total = None
            for m in range(count):
                tile = m_ref[m, f, l]
                total = tile if total is None else total + tile
                packs[m] = put_slot(packs[m], tile, l)
                edges_of(tile, (m * mf + f) * levels + l)
            sum_ref[f, l] = total
        for m in range(count):
            pm_ref[m * mf + f] = packs[m]
    base = count * mf
    packed = jnp.zeros((rows, LANES), F32)
    for l in range(levels):
        tile = d_ref[l]
        packed = put_slot(packed, tile, l)
        edges_of(tile, base * levels + l)
    pm_ref[base] = packed
    tile = r_ref[...]
    pm_ref[base + 1] = put_slot(jnp.zeros((rows, LANES), F32), tile, 0)
    edges_of(tile, (base + 1) * levels)


def pack(control, members, diffusivity, rotation):
    fields, clevels, crows, ccols = control.shape
    count, mf, levels, rows, cols = members.shape
    tiles = (count * mf + 1) * levels + 1
    shapes = (
        (1, crows, LANES),
        (count * mf + 2, rows, LANES),
        (mf, levels, rows, cols),
        (tiles, H, cols),
        (tiles, H, cols),
        (fields, clevels, H, ccols),
        (fields, clevels, H, ccols),
    )
    return pl.pallas_call(
        pack_kernel,
        out_shape=[jax.ShapeDtypeStruct(s, F32) for s in shapes],
        cost_estimate=cost(4 * members.size, 6 * members.size),
        name="pack",
    )(control, members, diffusivity, rotation)


def control_kernel(same, c_ref, nx_ref, px_ref, mean_ref, *rest):
    sides = rest[:3] if same else rest[:6]
    out_ref, corr_ref, pcorr_ref = rest[-3:]
    fields, _, rows, cols = c_ref.shape
    clevels = pl.num_programs(0)
    level = pl.program_id(0)
    full = cols + LANES
    body = []
    left = jnp.concatenate([sides[0][0], sides[1][0], sides[2][0]], axis=0)
    right = left if same else jnp.concatenate([sides[3][0], sides[4][0], sides[5][0]], axis=0)
    for f in range(fields):
        own = jnp.concatenate([c_ref[f, 0], nx_ref[f, 0], px_ref[f, 0]], axis=0)
        side = side_block(left, right, f * clevels + level)
        body.append(jnp.concatenate([own, side], axis=1))
    height = rows + 2 * H
    for _ in range(CSTEPS):
        a = body[0] * (0.5 * step_control)
        b = body[1] * (0.5 * step_control)
        new = []
        for f in body:
            ux = pltpu.roll(f, height - 1, 0)
            lx = pltpu.roll(f, 1, 0)
            uy = pltpu.roll(f, full - 1, 1)
            ly = pltpu.roll(f, 1, 1)
            lap = (ux + lx) + (uy + ly) - 4.0 * f
            new.append(f + ((step_control * viscosity) * lap - a * (ux - lx) - b * (uy - ly)))
        body = new
    half_x, half_y = rows // 2, cols // 2
    pick_y = (
        lax.broadcasted_iota(jnp.int32, (cols, half_y), 0) // 2
        == lax.broadcasted_iota(jnp.int32, (cols, half_y), 1)
    ).astype(F32)
    pick_x = (
        lax.broadcasted_iota(jnp.int32, (half_x, rows), 1) // 2
        == lax.broadcasted_iota(jnp.int32, (half_x, rows), 0)
    ).astype(F32)
    for f in range(fields):
        field = body[f][:rows, :cols]
        out_ref[f, 0] = field
        t = jnp.dot(field, pick_y, precision=lax.Precision.HIGHEST, preferred_element_type=F32)
        t = jnp.dot(pick_x, t, precision=lax.Precision.HIGHEST, preferred_element_type=F32)
        corr = 0.25 * t - mean_ref[f, 0]
        corr_ref[f, 0] = corr
        pcorr_ref[f] = put_slot(pcorr_ref[f], corr, level)


def control_call(control, nx, px, mean, sides):
    fields, clevels, crows, ccols = control.shape
    rows, cols = crows // 2, ccols // 2
    spec = lambda r, c: pl.BlockSpec((fields, 1, r, c), lambda l: (0, l, 0, 0))
    return pl.pallas_call(
        functools.partial(control_kernel, len(sides) == 3),
        grid=(clevels,),
        in_specs=[spec(crows, ccols), spec(H, ccols), spec(H, ccols), spec(rows, cols)]
        + [whole(s.shape) for s in sides],
        out_specs=[spec(crows, ccols), spec(rows, cols), whole((fields, rows, cols))],
        out_shape=[
            jax.ShapeDtypeStruct(control.shape, F32),
            jax.ShapeDtypeStruct(mean.shape, F32),
            jax.ShapeDtypeStruct((fields, rows, cols), F32),
        ],
        cost_estimate=cost(200 * control.size, 12 * control.size),
        name="control",
    )(control, nx, px, mean, *sides)


def member_kernel(same, slot_ref, m_ref, nm_ref, pm_ref, d_ref, nd_ref, pd_ref, r_ref, nr_ref, pr_ref, *rest):
    out_ref = rest[-1]
    group = 3 if same else 6
    ms, ks = rest[:group], rest[group : 2 * group]
    count, fields, _, rows, cols = m_ref.shape
    level = pl.program_id(0)
    height, full = rows + 2 * H, cols + LANES

    def extend(own, sides, g, slot):
        left = jnp.concatenate([sides[0][g], sides[1][g], sides[2][g]], axis=0)
        right = left
        if not same:
            right = jnp.concatenate([sides[3][g], sides[4][g], sides[5][g]], axis=0)
        own = jnp.concatenate(own, axis=0)
        return jnp.concatenate([own, side_block(left, right, slot)], axis=1)

    up_x = lambda f: pltpu.roll(f, height - 1, 0)
    low_x = lambda f: pltpu.roll(f, 1, 0)
    up_y = lambda f: pltpu.roll(f, full - 1, 1)
    low_y = lambda f: pltpu.roll(f, 1, 1)
    kappa = extend([d_ref[0], nd_ref[0], pd_ref[0]], ks, 0, slot_ref[0] + level)
    spin = step_member * extend([r_ref[...], nr_ref[0], pr_ref[0]], ks, 1, 0 * level)
    east = (0.5 * step_member) * (kappa + up_x(kappa))
    north = (0.5 * step_member) * (kappa + up_y(kappa))
    for m in range(count):
        pair = []
        for f in range(fields):
            own = [m_ref[m, f, 0], nm_ref[m, f, 0], pm_ref[m, f, 0]]
            pair.append(extend(own, ms, m * fields + f, level))
        p, q = pair
        for _ in range(MSTEPS):
            moved = []
            for f in (p, q):
                fx = east * (up_x(f) - f)
                fy = north * (up_y(f) - f)
                moved.append(f + ((fx - low_x(fx)) + (fy - low_y(fy))))
            p, q = moved[0] - spin * q, moved[1] + spin * p
        out_ref[m, 0, 0] = p[:rows, :cols]
        out_ref[m, 1, 0] = q[:rows, :cols]


def member_call(slot, members, nm, pm, diffusivity, nd, pd, rotation, nr, pr, msides, ksides, name):
    count, fields, levels, rows, cols = members.shape
    mspec = lambda r: pl.BlockSpec((count, fields, 1, r, cols), lambda l, s: (0, 0, l, 0, 0))
    dspec = lambda r: pl.BlockSpec((1, r, cols), lambda l, s: (s[0] + l, 0, 0))
    return pl.pallas_call(
        functools.partial(member_kernel, len(msides) == 3),
        grid_spec=pltpu.PrefetchScalarGridSpec(
            num_scalar_prefetch=1,
            grid=(levels,),
            in_specs=[mspec(rows), mspec(H), mspec(H), dspec(rows), dspec(H), dspec(H)]
            + [whole(a.shape) for a in (rotation, nr, pr, *msides, *ksides)],
            out_specs=mspec(rows),
        ),
        out_shape=jax.ShapeDtypeStruct(members.shape, F32),
        cost_estimate=cost(200 * members.size, 8 * members.size),
        name=name,
    )(slot, members, nm, pm, diffusivity, nd, pd, rotation, nr, pr, *msides, *ksides)


def from_next(x, axis):
    n = lax.axis_size(axis)
    return lax.ppermute(x, axis, [((i + 1) % n, i) for i in range(n)])


def from_prev(x, axis):
    n = lax.axis_size(axis)
    return lax.ppermute(x, axis, [(i, (i + 1) % n) for i in range(n)])


def y_sides(packed):
    if lax.axis_size("gy") == 2:
        return [from_next(packed, "gy")]
    return [from_prev(packed, "gy"), from_next(packed, "gy")]


def with_rows(packs):
    out = []
    for p in packs:
        out += [p, from_next(p[:, :H], "gx"), from_prev(p[:, -H:], "gx")]
    return out


def per_device(control, members, diffusivity, rotation):
    count, fields, levels, rows, cols = members.shape
    clevels = control.shape[1]
    n = lax.axis_size("mem")
    me = lax.axis_index("mem")
    pc, pm, sums, hm, tm, hc, tc = pack(control, members, diffusivity, rotation)
    nc, prc = from_next(hc, "gx"), from_prev(tc, "gx")
    csides = with_rows(y_sides(pc))
    nm, prm = from_next(hm, "gx"), from_prev(tm, "gx")
    sides = with_rows(y_sides(pm))
    chunk = lambda k: lax.dynamic_slice_in_dim(sums, lax.rem(me + k, n) * clevels, clevels, 1)
    ring = lambda x, k: lax.ppermute(x, "mem", [(i, (i + k) % n) for i in range(n)])
    total = chunk(0)
    for k in range(1, n):
        total = total + ring(chunk(k), k)
    mean = total / (count * n)
    control_final, corr, pcorr = control_call(control, nc, prc, mean, csides)

    base = count * fields
    tiles = base * levels
    ksides = [s[base:] for s in sides]
    split = lambda x, a, b: x[a:b]
    nd, prd = nm[tiles : tiles + levels], prm[tiles : tiles + levels]
    nr, prr = nm[tiles + levels :], prm[tiles + levels :]
    shape = (count, fields, levels, H, cols)
    free = member_call(
        jnp.zeros((1,), jnp.int32), members, nm[:tiles].reshape(shape), prm[:tiles].reshape(shape),
        diffusivity, nd, prd, rotation, nr, prr, [s[:base] for s in sides], ksides, "members",
    )
    ncorr, prcorr = from_next(corr[:, :, :H], "gx"), from_prev(corr[:, :, rows - H :], "gx")
    corr_sides = with_rows(y_sides(pcorr))
    shift = member_call(
        (me * clevels)[None].astype(jnp.int32), corr[None], ncorr[None], prcorr[None],
        diffusivity, nd, prd, rotation, nr, prr, corr_sides, ksides, "correction",
    )[0]
    gathered = jnp.zeros((fields, levels, rows, cols), F32)
    for k in range(n):
        piece = shift if k == 0 else ring(shift, n - k)
        gathered = lax.dynamic_update_slice_in_dim(
            gathered, piece, lax.rem(me + k, n) * clevels, 1
        )
    return (control_final, free + gathered[None])


def solution(mesh):
    in_specs = (
        P(None, "mem", "gx", "gy"),
        P("mem", None, None, "gx", "gy"),
        P(None, "gx", "gy"),
        P("gx", "gy"),
    )
    out_specs = (P(None, "mem", "gx", "gy"), P("mem", None, None, "gx", "gy"))
    return jax.shard_map(
        per_device, mesh=mesh, in_specs=in_specs, out_specs=out_specs, check_vma=False
    )
```

```python
import functools

import jax
import jax.numpy as jnp
from jax import lax
from jax.experimental import pallas as pl
from jax.experimental.pallas import tpu as pltpu
from jax.sharding import PartitionSpec as P

CSTEPS = 4
MSTEPS = 4
H = 4
SLOT = 2 * H
LANES = 128

step_control = 0.15
viscosity = 0.5
step_member = 0.5
F32 = jnp.float32


def lane_ids(rows):
    return lax.broadcasted_iota(jnp.int32, (rows, LANES), 1)


def put_slot(packed, edges, slot):
    shift = H + SLOT * slot
    if not isinstance(slot, int):
        shift = lax.rem(shift, LANES)
    rolled = pltpu.roll(edges, shift, 1)
    ids = lane_ids(edges.shape[0])
    inside = (ids >= SLOT * slot) & (ids < SLOT * slot + SLOT)
    return jnp.where(inside, rolled, packed)


def side_block(left, right, slot):
    shift = lax.rem(2 * LANES - SLOT * slot - H, LANES)
    after = pltpu.roll(right, shift, 1)
    if left is right:
        return after
    before = pltpu.roll(left, shift, 1)
    return jnp.where(lane_ids(after.shape[0]) < LANES // 2, after, before)


def fused_kernel(
    copies, c_ref, m_ref, d_ref, r_ref, cf_ref, mf_ref,
    hc, tc, nc, prc, hm, tm, nm, prm, yc, ym, yc_in, ym_in, ccor, mcor, ccor_in, mcor_in,
    sums, sums_in, corr, hcorr, tcorr, ncorr, prcorr, ycorr, ycorr_in, kcor, kcor_in,
    shift, shift_in, send_sem, recv_sem,
):
    fields, clevels, crows, ccols = c_ref.shape
    count, _, levels, rows, cols = m_ref.shape
    base = count * fields
    nx, ny, n = lax.axis_size("gx"), lax.axis_size("gy"), lax.axis_size("mem")
    x, y, me = lax.axis_index("gx"), lax.axis_index("gy"), lax.axis_index("mem")
    two = ny > 2
    nsides = 2 if two else 1
    x_next, x_prev = {"gx": lax.rem(x + 1, nx)}, {"gx": lax.rem(x + nx - 1, nx)}
    y_next, y_prev = {"gy": lax.rem(y + 1, ny)}, {"gy": lax.rem(y + ny - 1, ny)}
    peers = [{"mem": lax.rem(me + k, n)} for k in range(1, n)]
    mesh_id = pl.DeviceIdType.MESH
    pending = []

    def send(src, dst, target):
        k = len(pending)
        copy = pltpu.make_async_remote_copy(
            src_ref=src, dst_ref=dst, send_sem=send_sem.at[k], recv_sem=recv_sem.at[k],
            device_id=target, device_id_type=mesh_id,
        )
        copy.start()
        pending.append(copy)
        return copy

    def landed(group):
        for copy in group:
            copy.wait_recv()

    def send_y(src, dst):
        group = [send(src, dst.at[0], y_next)]
        if two:
            group.append(send(src, dst.at[1], y_prev))
        return group

    def send_x(first, last, from_next, from_prev):
        return [send(first, from_next, x_prev), send(last, from_prev, x_next)]

    def send_corners(got, buf, buf_in):
        group = []
        for side in range(nsides):
            for g in range(got.shape[1]):
                tile = got[side, g]
                buf[side, 0, g] = tile[:H]
                buf[side, 1, g] = tile[tile.shape[0] - H :]
            group += send_x(
                buf.at[side, 0], buf.at[side, 1], buf_in.at[side, 0], buf_in.at[side, 1]
            )
        return group

    barrier = pltpu.get_barrier_semaphore()
    greeted = [x_next, x_prev, y_next] + ([y_prev] if two else []) + peers
    for target in greeted:
        pl.semaphore_signal(barrier, inc=1, device_id=target, device_id_type=mesh_id)

    ids = lane_ids(crows)
    yc[...] = jnp.zeros_like(yc)
    ym[...] = jnp.zeros_like(ym)
    ycorr[...] = jnp.zeros_like(ycorr)

    @pl.loop(0, clevels)
    def _(l):
        for f in range(fields):
            first = c_ref[f, l, :, :LANES]
            last = c_ref[f, l, :, ccols - LANES :]
            t = f * clevels + l
            yc[0] = put_slot(yc[0], jnp.where(ids < LANES // 2, first, last), t)
            hc[t] = c_ref[f, l, :H]
            tc[t] = c_ref[f, l, crows - H :]

    pl.semaphore_wait(barrier, len(greeted))
    got_yc = send_y(yc, yc_in)
    got_xc = send_x(hc, tc, nc, prc)

    @pl.loop(0, levels)
    def _(l):
        for f in range(fields):
            total = None
            for m in range(count):
                tile = m_ref[m, f, l]
                total = tile if total is None else total + tile
                g = m * fields + f
                ym[g] = put_slot(ym[g], tile, l)
                hm[g * levels + l] = tile[:H]
                tm[g * levels + l] = tile[rows - H :]
            sums[l, f] = total
        tile = d_ref[l]
        ym[base] = put_slot(ym[base], tile, l)
        hm[base * levels + l] = tile[:H]
        tm[base * levels + l] = tile[rows - H :]

    tile = r_ref[...]
    ym[base + 1] = put_slot(jnp.zeros((rows, LANES), F32), tile, 0)
    hm[(base + 1) * levels] = tile[:H]
    tm[(base + 1) * levels] = tile[rows - H :]
    got_ym = send_y(ym, ym_in)
    got_xm = send_x(hm, tm, nm, prm)
    got_sum = []
    for k in range(1, n):
        owner = lax.rem(me + k, n)
        got_sum.append(send(sums.at[pl.ds(owner * clevels, clevels)], sums_in.at[k - 1], peers[k - 1]))

    landed(got_yc)
    got_cc = send_corners(yc_in, ccor, ccor_in)
    landed(got_xc)
    landed(got_cc)

    def side_values(body, corners, g):
        out = [
            jnp.concatenate([body[s, g], corners[s, 0, g], corners[s, 1, g]], axis=0)
            for s in range(nsides)
        ]
        return out[0], out[-1]

    half_x, half_y = crows // 2, ccols // 2
    height, full = crows + 2 * H, ccols + LANES

    def control_level(l):
        left, right = side_values(yc_in, ccor_in, 0)
        body = []
        for f in range(fields):
            t = f * clevels + l
            own = jnp.concatenate([c_ref[f, l], nc[t], prc[t]], axis=0)
            body.append(jnp.concatenate([own, side_block(left, right, t)], axis=1))
        for _ in range(CSTEPS):
            a = body[0] * (0.5 * step_control)
            b = body[1] * (0.5 * step_control)
            new = []
            for f in body:
                ux = pltpu.roll(f, height - 1, 0)
                lx = pltpu.roll(f, 1, 0)
                uy = pltpu.roll(f, full - 1, 1)
                ly = pltpu.roll(f, 1, 1)
                lap = (ux + lx) + (uy + ly) - 4.0 * f
                new.append(f + ((step_control * viscosity) * lap - a * (ux - lx) - b * (uy - ly)))
            body = new
        pick_y = (
            lax.broadcasted_iota(jnp.int32, (ccols, half_y), 0) // 2
            == lax.broadcasted_iota(jnp.int32, (ccols, half_y), 1)
        ).astype(F32)
        pick_x = (
            lax.broadcasted_iota(jnp.int32, (half_x, crows), 1) // 2
            == lax.broadcasted_iota(jnp.int32, (half_x, crows), 0)
        ).astype(F32)
        for f in range(fields):
            field = body[f][:crows, :ccols]
            cf_ref[f, l] = field
            t = jnp.dot(field, pick_y, precision=lax.Precision.HIGHEST, preferred_element_type=F32)
            t = jnp.dot(pick_x, t, precision=lax.Precision.HIGHEST, preferred_element_type=F32)
            corr[l, f] = 0.25 * t

    landed(got_ym)
    got_mc = send_corners(ym_in, mcor, mcor_in)
    pl.loop(0, clevels)(control_level)
    landed(got_sum)

    @pl.loop(0, clevels)
    def _(l):
        for f in range(fields):
            total = sums[me * clevels + l, f]
            for k in range(n - 1):
                total = total + sums_in[k, l, f]
            tile = corr[l, f] - total * (1.0 / (count * n))
            corr[l, f] = tile
            ycorr[f] = put_slot(ycorr[f], tile, l)
            hcorr[f * clevels + l] = tile[:H]
            tcorr[f * clevels + l] = tile[rows - H :]

    got_yk = send_y(ycorr, ycorr_in)
    got_xk = send_x(hcorr, tcorr, ncorr, prcorr)
    landed(got_xm)
    landed(got_mc)

    mheight, mfull = rows + 2 * H, cols + LANES
    up_x = lambda f: pltpu.roll(f, mheight - 1, 0)
    low_x = lambda f: pltpu.roll(f, 1, 0)
    up_y = lambda f: pltpu.roll(f, mfull - 1, 1)
    low_y = lambda f: pltpu.roll(f, 1, 1)

    def extend(own, after, before, sides, slot):
        own = jnp.concatenate([own, after, before], axis=0)
        return jnp.concatenate([own, side_block(*sides, slot)], axis=1)

    def weights(l):
        t = base * levels + l
        kappa = extend(d_ref[l], nm[t], prm[t], side_values(ym_in, mcor_in, base), l)
        t = (base + 1) * levels
        spin = extend(r_ref[...], nm[t], prm[t], side_values(ym_in, mcor_in, base + 1), 0)
        east = (0.5 * step_member) * (kappa + up_x(kappa))
        north = (0.5 * step_member) * (kappa + up_y(kappa))
        return east, north, step_member * spin

    def steps(p, q, east, north, spin):
        for _ in range(MSTEPS):
            moved = []
            for f in (p, q):
                fx = east * (up_x(f) - f)
                fy = north * (up_y(f) - f)
                moved.append(f + ((fx - low_x(fx)) + (fy - low_y(fy))))
            p, q = moved[0] - spin * q, moved[1] + spin * p
        return p[:rows, :cols], q[:rows, :cols]

    def member_level(l):
        w = weights(l)
        for m in range(count):
            pair = []
            for f in range(fields):
                g = m * fields + f
                t = g * levels + l
                pair.append(extend(m_ref[m, f, l], nm[t], prm[t], side_values(ym_in, mcor_in, g), l))
            mf_ref[m, 0, l], mf_ref[m, 1, l] = steps(*pair, *w)

    def correction_level(l):
        w = weights(me * clevels + l)
        pair = []
        for f in range(fields):
            t = f * clevels + l
            pair.append(extend(corr[l, f], ncorr[t], prcorr[t], side_values(ycorr_in, kcor_in, f), l))
        shift[l, 0], shift[l, 1] = steps(*pair, *w)

    cut_a, cut_b = (3 * levels) // 16, (6 * levels) // 16
    pl.loop(0, cut_a)(member_level)
    landed(got_yk)
    got_kc = send_corners(ycorr_in, kcor, kcor_in)
    pl.loop(cut_a, cut_b)(member_level)
    landed(got_xk)
    landed(got_kc)
    pl.loop(0, clevels)(correction_level)
    got_shift = [send(shift, shift_in.at[k], peers[k]) for k in range(n - 1)]
    pl.loop(cut_b, levels)(member_level)

    def add(piece, owner):
        @pl.loop(0, clevels)
        def _(l):
            for f in range(fields):
                tile = piece[l, f]
                for m in range(count):
                    at = owner * clevels + l
                    mf_ref[m, f, at] = mf_ref[m, f, at] + tile

    add(shift, me)
    for k in range(n - 1):
        landed([got_shift[k]])
        add(shift_in.at[k], lax.rem(me + n - 1 - k, n))
    for copy in pending:
        copy.wait_send()
    assert len(pending) == copies


def per_device(control, members, diffusivity, rotation):
    fields, clevels, crows, ccols = control.shape
    count, _, levels, rows, cols = members.shape
    base = count * fields
    tiles = (base + 1) * levels + 1
    n = lax.axis_size("mem")
    ns = 2 if lax.axis_size("gy") > 2 else 1
    copies = 3 * (ns + 2 + 2 * ns) + 2 * (n - 1)
    vmem = lambda *shape: pltpu.VMEM(shape, F32)
    scratch = (
        [vmem(fields * clevels, H, ccols)] * 4
        + [vmem(tiles, H, cols)] * 4
        + [vmem(1, crows, LANES), vmem(base + 2, rows, LANES)]
        + [vmem(ns, 1, crows, LANES), vmem(ns, base + 2, rows, LANES)]
        + [vmem(ns, 2, 1, H, LANES), vmem(ns, 2, base + 2, H, LANES)] * 2
        + [vmem(levels, fields, rows, cols), vmem(n - 1, clevels, fields, rows, cols)]
        + [vmem(clevels, fields, rows, cols)]
        + [vmem(fields * clevels, H, cols)] * 4
        + [vmem(fields, rows, LANES), vmem(ns, fields, rows, LANES)]
        + [vmem(ns, 2, fields, H, LANES)] * 2
        + [vmem(clevels, fields, rows, cols), vmem(n - 1, clevels, fields, rows, cols)]
        + [pltpu.SemaphoreType.DMA((copies,))] * 2
    )
    return pl.pallas_call(
        functools.partial(fused_kernel, copies),
        in_specs=[pl.BlockSpec(memory_space=pltpu.VMEM)] * 4,
        out_specs=[pl.BlockSpec(memory_space=pltpu.VMEM)] * 2,
        out_shape=[
            jax.ShapeDtypeStruct(control.shape, F32),
            jax.ShapeDtypeStruct(members.shape, F32),
        ],
        scratch_shapes=scratch,
        compiler_params=pltpu.CompilerParams(collective_id=0, has_side_effects=True),
        name="fused",
    )(control, members, diffusivity, rotation)


def solution(mesh):
    in_specs = (
        P(None, "mem", "gx", "gy"),
        P("mem", None, None, "gx", "gy"),
        P(None, "gx", "gy"),
        P("gx", "gy"),
    )
    out_specs = (P(None, "mem", "gx", "gy"), P("mem", None, None, "gx", "gy"))
    return jax.shard_map(
        per_device, mesh=mesh, in_specs=in_specs, out_specs=out_specs, check_vma=False
    )
```

```python
import functools

import jax
import jax.numpy as jnp
from jax import lax
from jax.experimental import pallas as pl
from jax.experimental.pallas import tpu as pltpu
from jax.sharding import PartitionSpec as P

CSTEPS = 4
MSTEPS = 4
H = 4
SLOT = 2 * H
STRIP = 4 * H
LANES = 128

step_control = 0.15
viscosity = 0.5
step_member = 0.5
F32 = jnp.float32


def lane_ids(rows):
    return lax.broadcasted_iota(jnp.int32, (rows, LANES), 1)


def put_slot(packed, edges, slot):
    shift = H + SLOT * slot
    if not isinstance(slot, int):
        shift = lax.rem(shift, LANES)
    rolled = pltpu.roll(edges, shift, 1)
    ids = lane_ids(edges.shape[0])
    inside = (ids >= SLOT * slot) & (ids < SLOT * slot + SLOT)
    return jnp.where(inside, rolled, packed)


def side_block(left, right, slot):
    shift = lax.rem(2 * LANES - SLOT * slot - H, LANES)
    after = pltpu.roll(right, shift, 1)
    if left is right:
        return after
    before = pltpu.roll(left, shift, 1)
    return jnp.where(lane_ids(after.shape[0]) < LANES // 2, after, before)


def fused_kernel(
    copies, c_ref, m_ref, d_ref, r_ref, cf_ref, mf_ref,
    hc, tc, nc, prc, hm, tm, nm, prm, yc, ym, yc_in, ym_in, ccor, mcor, ccor_in, mcor_in,
    sums, sums_in, corr, hcorr, tcorr, ncorr, prcorr, ycorr, ycorr_in, kcor, kcor_in,
    shift, shift_in, send_sem, recv_sem,
):
    fields, clevels, crows, ccols = c_ref.shape
    count, _, levels, rows, cols = m_ref.shape
    base = count * fields
    nx, ny, n = lax.axis_size("gx"), lax.axis_size("gy"), lax.axis_size("mem")
    x, y, me = lax.axis_index("gx"), lax.axis_index("gy"), lax.axis_index("mem")
    two = ny > 2
    nsides = 2 if two else 1
    x_next, x_prev = {"gx": lax.rem(x + 1, nx)}, {"gx": lax.rem(x + nx - 1, nx)}
    y_next, y_prev = {"gy": lax.rem(y + 1, ny)}, {"gy": lax.rem(y + ny - 1, ny)}
    peers = [{"mem": lax.rem(me + k, n)} for k in range(1, n)]
    mesh_id = pl.DeviceIdType.MESH
    pending = []

    def send(src, dst, target):
        k = len(pending)
        copy = pltpu.make_async_remote_copy(
            src_ref=src, dst_ref=dst, send_sem=send_sem.at[k], recv_sem=recv_sem.at[k],
            device_id=target, device_id_type=mesh_id,
        )
        copy.start()
        pending.append(copy)
        return copy

    def landed(group):
        for copy in group:
            copy.wait_recv()

    def send_y(src, dst):
        group = [send(src, dst.at[0], y_next)]
        if two:
            group.append(send(src, dst.at[1], y_prev))
        return group

    def send_x(first, last, from_next, from_prev):
        return [send(first, from_next, x_prev), send(last, from_prev, x_next)]

    def send_corners(got, buf, buf_in):
        group = []
        for side in range(nsides):
            for g in range(got.shape[1]):
                tile = got[side, g]
                buf[side, 0, g] = tile[:H]
                buf[side, 1, g] = tile[tile.shape[0] - H :]
            group += send_x(
                buf.at[side, 0], buf.at[side, 1], buf_in.at[side, 0], buf_in.at[side, 1]
            )
        return group

    barrier = pltpu.get_barrier_semaphore()
    greeted = [x_next, x_prev, y_next] + ([y_prev] if two else []) + peers
    for target in greeted:
        pl.semaphore_signal(barrier, inc=1, device_id=target, device_id_type=mesh_id)

    ids = lane_ids(crows)
    yc[...] = jnp.zeros_like(yc)
    ym[...] = jnp.zeros_like(ym)
    ycorr[...] = jnp.zeros_like(ycorr)

    @pl.loop(0, clevels)
    def _(l):
        for f in range(fields):
            first = c_ref[f, l, :, :LANES]
            last = c_ref[f, l, :, ccols - LANES :]
            t = f * clevels + l
            yc[0] = put_slot(yc[0], jnp.where(ids < LANES // 2, first, last), t)
            hc[t] = c_ref[f, l, :H]
            tc[t] = c_ref[f, l, crows - H :]

    pl.semaphore_wait(barrier, len(greeted))
    got_yc = send_y(yc, yc_in)
    got_xc = send_x(hc, tc, nc, prc)

    @pl.loop(0, levels)
    def _(l):
        for f in range(fields):
            total = None
            for m in range(count):
                tile = m_ref[m, f, l]
                total = tile if total is None else total + tile
                g = m * fields + f
                ym[g] = put_slot(ym[g], tile, l)
                hm[g * levels + l] = tile[:H]
                tm[g * levels + l] = tile[rows - H :]
            sums[l, f] = total
        tile = d_ref[l]
        ym[base] = put_slot(ym[base], tile, l)
        hm[base * levels + l] = tile[:H]
        tm[base * levels + l] = tile[rows - H :]

    tile = r_ref[...]
    ym[base + 1] = put_slot(jnp.zeros((rows, LANES), F32), tile, 0)
    hm[(base + 1) * levels] = tile[:H]
    tm[(base + 1) * levels] = tile[rows - H :]
    got_ym = send_y(ym, ym_in)
    got_xm = send_x(hm, tm, nm, prm)
    got_sum = []
    for k in range(1, n):
        owner = lax.rem(me + k, n)
        got_sum.append(send(sums.at[pl.ds(owner * clevels, clevels)], sums_in.at[k - 1], peers[k - 1]))

    landed(got_yc)
    got_cc = send_corners(yc_in, ccor, ccor_in)
    landed(got_xc)
    landed(got_cc)

    def side_values(body, corners, g):
        out = [
            jnp.concatenate([body[s, g], corners[s, 0, g], corners[s, 1, g]], axis=0)
            for s in range(nsides)
        ]
        return out[0], out[-1]

    half_x, half_y = crows // 2, ccols // 2
    height, full = crows + 2 * H, ccols + LANES

    def control_level(l):
        left, right = side_values(yc_in, ccor_in, 0)
        body = []
        for f in range(fields):
            t = f * clevels + l
            own = jnp.concatenate([c_ref[f, l], nc[t], prc[t]], axis=0)
            body.append(jnp.concatenate([own, side_block(left, right, t)], axis=1))
        for _ in range(CSTEPS):
            a = body[0] * (0.5 * step_control)
            b = body[1] * (0.5 * step_control)
            new = []
            for f in body:
                ux = pltpu.roll(f, height - 1, 0)
                lx = pltpu.roll(f, 1, 0)
                uy = pltpu.roll(f, full - 1, 1)
                ly = pltpu.roll(f, 1, 1)
                lap = (ux + lx) + (uy + ly) - 4.0 * f
                new.append(f + ((step_control * viscosity) * lap - a * (ux - lx) - b * (uy - ly)))
            body = new
        pick_y = (
            lax.broadcasted_iota(jnp.int32, (ccols, half_y), 0) // 2
            == lax.broadcasted_iota(jnp.int32, (ccols, half_y), 1)
        ).astype(F32)
        pick_x = (
            lax.broadcasted_iota(jnp.int32, (half_x, crows), 1) // 2
            == lax.broadcasted_iota(jnp.int32, (half_x, crows), 0)
        ).astype(F32)
        for f in range(fields):
            field = body[f][:crows, :ccols]
            cf_ref[f, l] = field
            t = jnp.dot(field, pick_y, precision=lax.Precision.HIGHEST, preferred_element_type=F32)
            t = jnp.dot(pick_x, t, precision=lax.Precision.HIGHEST, preferred_element_type=F32)
            corr[l, f] = 0.25 * t

    landed(got_ym)
    got_mc = send_corners(ym_in, mcor, mcor_in)
    pl.loop(0, clevels)(control_level)
    landed(got_sum)

    @pl.loop(0, clevels)
    def _(l):
        for f in range(fields):
            total = sums[me * clevels + l, f]
            for k in range(n - 1):
                total = total + sums_in[k, l, f]
            tile = corr[l, f] - total * (1.0 / (count * n))
            corr[l, f] = tile
            ycorr[f] = put_slot(ycorr[f], tile, l)
            hcorr[f * clevels + l] = tile[:H]
            tcorr[f * clevels + l] = tile[rows - H :]

    got_yk = send_y(ycorr, ycorr_in)
    got_xk = send_x(hcorr, tcorr, ncorr, prcorr)
    landed(got_xm)
    landed(got_mc)

    mheight = rows + 2 * H
    lane = lane_ids(mheight)
    turn = lambda f, by: pltpu.roll(f, by, 1)
    up_x = lambda f: pltpu.roll(f, mheight - 1, 0)
    low_x = lambda f: pltpu.roll(f, 1, 0)

    def up_y(f, strip, g):
        beyond = turn(strip, (2 * LANES - 1 - (STRIP * g + 3 * H)) % LANES)
        return jnp.where(lane == LANES - 1, beyond, turn(f, LANES - 1))

    def low_y(f, strip, g):
        return jnp.where(lane == 0, turn(strip, (LANES - (STRIP * g + H - 1)) % LANES), turn(f, 1))

    def with_strip(strip, own, sides, slot, g):
        at = lane - STRIP * g
        from_slot = lambda to: lax.rem(to + 2 * LANES - SLOT * slot, LANES)
        parts = (
            turn(sides[0], from_slot(STRIP * g)),
            turn(own, (STRIP * g + H) % LANES),
            turn(own, (STRIP * g + 3 * H) % LANES),
            turn(sides[1], from_slot(STRIP * g + 2 * H)),
        )
        for k, part in enumerate(parts):
            strip = jnp.where((at >= k * H) & (at < (k + 1) * H), part, strip)
        return strip

    def everywhere(strip):
        by = STRIP
        while by < LANES:
            strip = strip + turn(strip, by)
            by *= 2
        return strip

    def stack_rows(own, after, before):
        return jnp.concatenate([own, after, before], axis=0)

    blank = jnp.zeros((mheight, LANES), F32)
    odd = lax.rem(lane // STRIP, 2) == 1

    def weights(l):
        t = base * levels + l
        kappa = stack_rows(d_ref[l], nm[t], prm[t])
        kstrip = with_strip(blank, kappa, side_values(ym_in, mcor_in, base), l, 0)
        t = (base + 1) * levels
        spin = stack_rows(r_ref[...], nm[t], prm[t])
        sstrip = with_strip(blank, spin, side_values(ym_in, mcor_in, base + 1), 0, 0)
        half = 0.5 * step_member
        east, north = half * (kappa + up_x(kappa)), half * (kappa + up_y(kappa, kstrip, 0))
        kstrip = everywhere(kstrip)
        east_s, north_s = half * (kstrip + up_x(kstrip)), half * (kstrip + turn(kstrip, LANES - 1))
        sstrip = step_member * everywhere(sstrip)
        return east, north, step_member * spin, east_s, north_s, jnp.where(odd, sstrip, -sstrip)

    def steps(state, strip, w):
        east, north, spin, east_s, north_s, spin_s = w
        for step in range(MSTEPS):
            sy = north_s * (turn(strip, LANES - 1) - strip)
            moved = []
            for g, f in enumerate(state):
                fx = east * (up_x(f) - f)
                fy = north * (up_y(f, strip, g) - f)
                moved.append(f + ((fx - low_x(fx)) + (fy - low_y(fy, sy, g))))
            for g in range(0, len(state), 2):
                p, q = state[g], state[g + 1]
                moved[g] = moved[g] - spin * q
                moved[g + 1] = moved[g + 1] + spin * p
            if step < MSTEPS - 1:
                sx = east_s * (up_x(strip) - strip)
                other = jnp.where(odd, turn(strip, STRIP), turn(strip, LANES - STRIP))
                strip = strip + ((sx - low_x(sx)) + (sy - turn(sy, 1))) + spin_s * other
            state = moved
        return [f[:rows] for f in state]

    def member_level(l):
        state, strip = [], blank
        for g in range(base):
            t = g * levels + l
            own = stack_rows(m_ref[g // fields, g % fields, l], nm[t], prm[t])
            strip = with_strip(strip, own, side_values(ym_in, mcor_in, g), l, g)
            state.append(own)
        for g, f in enumerate(steps(state, strip, weights(l))):
            mf_ref[g // fields, g % fields, l] = f

    def correction_level(l):
        state, strip = [], blank
        for f in range(fields):
            t = f * clevels + l
            own = stack_rows(corr[l, f], ncorr[t], prcorr[t])
            strip = with_strip(strip, own, side_values(ycorr_in, kcor_in, f), l, f)
            state.append(own)
        for f, value in enumerate(steps(state, strip, weights(me * clevels + l))):
            shift[l, f] = value

    cut_a, cut_b = (3 * levels) // 16, (6 * levels) // 16
    pl.loop(0, cut_a)(member_level)
    landed(got_yk)
    got_kc = send_corners(ycorr_in, kcor, kcor_in)
    pl.loop(cut_a, cut_b)(member_level)
    landed(got_xk)
    landed(got_kc)
    pl.loop(0, clevels)(correction_level)
    got_shift = [send(shift, shift_in.at[k], peers[k]) for k in range(n - 1)]
    pl.loop(cut_b, levels)(member_level)

    def add(piece, owner):
        @pl.loop(0, clevels)
        def _(l):
            for f in range(fields):
                tile = piece[l, f]
                for m in range(count):
                    at = owner * clevels + l
                    mf_ref[m, f, at] = mf_ref[m, f, at] + tile

    add(shift, me)
    for k in range(n - 1):
        landed([got_shift[k]])
        add(shift_in.at[k], lax.rem(me + n - 1 - k, n))
    for copy in pending:
        copy.wait_send()
    assert len(pending) == copies


def per_device(control, members, diffusivity, rotation):
    fields, clevels, crows, ccols = control.shape
    count, _, levels, rows, cols = members.shape
    base = count * fields
    tiles = (base + 1) * levels + 1
    n = lax.axis_size("mem")
    ns = 2 if lax.axis_size("gy") > 2 else 1
    copies = 3 * (ns + 2 + 2 * ns) + 2 * (n - 1)
    vmem = lambda *shape: pltpu.VMEM(shape, F32)
    scratch = (
        [vmem(fields * clevels, H, ccols)] * 4
        + [vmem(tiles, H, cols)] * 4
        + [vmem(1, crows, LANES), vmem(base + 2, rows, LANES)]
        + [vmem(ns, 1, crows, LANES), vmem(ns, base + 2, rows, LANES)]
        + [vmem(ns, 2, 1, H, LANES), vmem(ns, 2, base + 2, H, LANES)] * 2
        + [vmem(levels, fields, rows, cols), vmem(n - 1, clevels, fields, rows, cols)]
        + [vmem(clevels, fields, rows, cols)]
        + [vmem(fields * clevels, H, cols)] * 4
        + [vmem(fields, rows, LANES), vmem(ns, fields, rows, LANES)]
        + [vmem(ns, 2, fields, H, LANES)] * 2
        + [vmem(clevels, fields, rows, cols), vmem(n - 1, clevels, fields, rows, cols)]
        + [pltpu.SemaphoreType.DMA((copies,))] * 2
    )
    return pl.pallas_call(
        functools.partial(fused_kernel, copies),
        in_specs=[pl.BlockSpec(memory_space=pltpu.VMEM)] * 4,
        out_specs=[pl.BlockSpec(memory_space=pltpu.VMEM)] * 2,
        out_shape=[
            jax.ShapeDtypeStruct(control.shape, F32),
            jax.ShapeDtypeStruct(members.shape, F32),
        ],
        scratch_shapes=scratch,
        compiler_params=pltpu.CompilerParams(collective_id=0, has_side_effects=True),
        name="fused",
    )(control, members, diffusivity, rotation)


def solution(mesh):
    in_specs = (
        P(None, "mem", "gx", "gy"),
        P("mem", None, None, "gx", "gy"),
        P(None, "gx", "gy"),
        P("gx", "gy"),
    )
    out_specs = (P(None, "mem", "gx", "gy"), P("mem", None, None, "gx", "gy"))
    return jax.shard_map(
        per_device, mesh=mesh, in_specs=in_specs, out_specs=out_specs, check_vma=False
    )
```

```python
import functools

import jax
import jax.numpy as jnp
from jax import lax
from jax.experimental import pallas as pl
from jax.experimental.pallas import tpu as pltpu
from jax.sharding import PartitionSpec as P

CSTEPS = 4
MSTEPS = 4
H = 4
SLOT = 2 * H
LANES = 128
EIGHT = 8

step_control = 0.15
viscosity = 0.5
step_member = 0.5
F32 = jnp.float32


def lane_ids(rows):
    return lax.broadcasted_iota(jnp.int32, (rows, LANES), 1)


def put_slot(packed, edges, slot):
    shift = H + SLOT * slot
    if not isinstance(slot, int):
        shift = lax.rem(shift, LANES)
    rolled = pltpu.roll(edges, shift, 1)
    ids = lane_ids(edges.shape[0])
    inside = (ids >= SLOT * slot) & (ids < SLOT * slot + SLOT)
    return jnp.where(inside, rolled, packed)


def side_block(left, right, slot):
    shift = lax.rem(2 * LANES - SLOT * slot - H, LANES)
    after = pltpu.roll(right, shift, 1)
    if left is right:
        return after
    before = pltpu.roll(left, shift, 1)
    return jnp.where(lane_ids(after.shape[0]) < LANES // 2, after, before)


def fused_kernel(
    copies, c_ref, m_ref, d_ref, r_ref, cf_ref, mf_ref,
    hc, tc, nc, prc, hm, tm, nm, prm, yc, ym, yc_in, ym_in, ccor, mcor, ccor_in, mcor_in,
    sums, sums_in, corr, hcorr, tcorr, ncorr, prcorr, ycorr, ycorr_in, kcor, kcor_in,
    shift, shift_in, stage, rowwise, faces, send_sem, recv_sem,
):
    fields, clevels, crows, ccols = c_ref.shape
    count, _, levels, rows, cols = m_ref.shape
    base = count * fields
    nx, ny, n = lax.axis_size("gx"), lax.axis_size("gy"), lax.axis_size("mem")
    x, y, me = lax.axis_index("gx"), lax.axis_index("gy"), lax.axis_index("mem")
    two = ny > 2
    nsides = 2 if two else 1
    x_next, x_prev = {"gx": lax.rem(x + 1, nx)}, {"gx": lax.rem(x + nx - 1, nx)}
    y_next, y_prev = {"gy": lax.rem(y + 1, ny)}, {"gy": lax.rem(y + ny - 1, ny)}
    peers = [{"mem": lax.rem(me + k, n)} for k in range(1, n)]
    mesh_id = pl.DeviceIdType.MESH
    pending = []

    def send(src, dst, target):
        k = len(pending)
        copy = pltpu.make_async_remote_copy(
            src_ref=src, dst_ref=dst, send_sem=send_sem.at[k], recv_sem=recv_sem.at[k],
            device_id=target, device_id_type=mesh_id,
        )
        copy.start()
        pending.append(copy)
        return copy

    def landed(group):
        for copy in group:
            copy.wait_recv()

    def send_y(src, dst):
        group = [send(src, dst.at[0], y_next)]
        if two:
            group.append(send(src, dst.at[1], y_prev))
        return group

    def send_x(first, last, from_next, from_prev):
        return [send(first, from_next, x_prev), send(last, from_prev, x_next)]

    def send_corners(got, buf, buf_in):
        group = []
        for side in range(nsides):
            for g in range(got.shape[1]):
                tile = got[side, g]
                buf[side, 0, g] = tile[:H]
                buf[side, 1, g] = tile[tile.shape[0] - H :]
            group += send_x(
                buf.at[side, 0], buf.at[side, 1], buf_in.at[side, 0], buf_in.at[side, 1]
            )
        return group

    barrier = pltpu.get_barrier_semaphore()
    greeted = [x_next, x_prev, y_next] + ([y_prev] if two else []) + peers
    for target in greeted:
        pl.semaphore_signal(barrier, inc=1, device_id=target, device_id_type=mesh_id)

    ids = lane_ids(crows)
    yc[...] = jnp.zeros_like(yc)
    ym[...] = jnp.zeros_like(ym)
    ycorr[...] = jnp.zeros_like(ycorr)

    @pl.loop(0, clevels)
    def _(l):
        for f in range(fields):
            first = c_ref[f, l, :, :LANES]
            last = c_ref[f, l, :, ccols - LANES :]
            t = f * clevels + l
            yc[0] = put_slot(yc[0], jnp.where(ids < LANES // 2, first, last), t)
            hc[t] = c_ref[f, l, :H]
            tc[t] = c_ref[f, l, crows - H :]

    pl.semaphore_wait(barrier, len(greeted))
    got_yc = send_y(yc, yc_in)
    got_xc = send_x(hc, tc, nc, prc)

    @pl.loop(0, levels)
    def _(l):
        for f in range(fields):
            total = None
            for m in range(count):
                tile = m_ref[m, f, l]
                total = tile if total is None else total + tile
                g = m * fields + f
                ym[g] = put_slot(ym[g], tile, l)
                hm[g * levels + l] = tile[:H]
                tm[g * levels + l] = tile[rows - H :]
            sums[l, f] = total
        tile = d_ref[l]
        ym[base] = put_slot(ym[base], tile, l)
        hm[base * levels + l] = tile[:H]
        tm[base * levels + l] = tile[rows - H :]

    tile = r_ref[...]
    ym[base + 1] = put_slot(jnp.zeros((rows, LANES), F32), tile, 0)
    hm[(base + 1) * levels] = tile[:H]
    tm[(base + 1) * levels] = tile[rows - H :]
    got_ym = send_y(ym, ym_in)
    got_xm = send_x(hm, tm, nm, prm)
    got_sum = []
    for k in range(1, n):
        owner = lax.rem(me + k, n)
        got_sum.append(send(sums.at[pl.ds(owner * clevels, clevels)], sums_in.at[k - 1], peers[k - 1]))

    landed(got_yc)
    got_cc = send_corners(yc_in, ccor, ccor_in)
    landed(got_xc)
    landed(got_cc)

    def side_values(body, corners, g):
        out = [
            jnp.concatenate([body[s, g], corners[s, 0, g], corners[s, 1, g]], axis=0)
            for s in range(nsides)
        ]
        return out[0], out[-1]

    half_x, half_y = crows // 2, ccols // 2
    height, full = crows + 2 * H, ccols + LANES

    def control_level(l):
        left, right = side_values(yc_in, ccor_in, 0)
        body = []
        for f in range(fields):
            t = f * clevels + l
            own = jnp.concatenate([c_ref[f, l], nc[t], prc[t]], axis=0)
            body.append(jnp.concatenate([own, side_block(left, right, t)], axis=1))
        for _ in range(CSTEPS):
            a = body[0] * (0.5 * step_control)
            b = body[1] * (0.5 * step_control)
            new = []
            for f in body:
                ux = pltpu.roll(f, height - 1, 0)
                lx = pltpu.roll(f, 1, 0)
                uy = pltpu.roll(f, full - 1, 1)
                ly = pltpu.roll(f, 1, 1)
                lap = (ux + lx) + (uy + ly) - 4.0 * f
                new.append(f + ((step_control * viscosity) * lap - a * (ux - lx) - b * (uy - ly)))
            body = new
        pick_y = (
            lax.broadcasted_iota(jnp.int32, (ccols, half_y), 0) // 2
            == lax.broadcasted_iota(jnp.int32, (ccols, half_y), 1)
        ).astype(F32)
        pick_x = (
            lax.broadcasted_iota(jnp.int32, (half_x, crows), 1) // 2
            == lax.broadcasted_iota(jnp.int32, (half_x, crows), 0)
        ).astype(F32)
        for f in range(fields):
            field = body[f][:crows, :ccols]
            cf_ref[f, l] = field
            t = jnp.dot(field, pick_y, precision=lax.Precision.HIGHEST, preferred_element_type=F32)
            t = jnp.dot(pick_x, t, precision=lax.Precision.HIGHEST, preferred_element_type=F32)
            corr[l, f] = 0.25 * t

    landed(got_ym)
    got_mc = send_corners(ym_in, mcor, mcor_in)
    pl.loop(0, clevels)(control_level)
    landed(got_sum)

    @pl.loop(0, clevels)
    def _(l):
        for f in range(fields):
            total = sums[me * clevels + l, f]
            for k in range(n - 1):
                total = total + sums_in[k, l, f]
            tile = corr[l, f] - total * (1.0 / (count * n))
            corr[l, f] = tile
            ycorr[f] = put_slot(ycorr[f], tile, l)
            hcorr[f * clevels + l] = tile[:H]
            tcorr[f * clevels + l] = tile[rows - H :]

    got_yk = send_y(ycorr, ycorr_in)
    got_xk = send_x(hcorr, tcorr, ncorr, prcorr)
    landed(got_xm)
    landed(got_mc)

    mheight, mfull = rows + 2 * H, cols + LANES
    up_x = lambda f: pltpu.roll(f, mheight - 1, 0)
    low_x = lambda f: pltpu.roll(f, 1, 0)
    up_y = lambda f: pltpu.roll(f, mfull - 1, 1)
    low_y = lambda f: pltpu.roll(f, 1, 1)

    def extend(own, after, before, sides, slot):
        own = jnp.concatenate([own, after, before], axis=0)
        return jnp.concatenate([own, side_block(*sides, slot)], axis=1)

    def weights(l):
        t = base * levels + l
        kappa = extend(d_ref[l], nm[t], prm[t], side_values(ym_in, mcor_in, base), l)
        t = (base + 1) * levels
        spin = extend(r_ref[...], nm[t], prm[t], side_values(ym_in, mcor_in, base + 1), 0)
        east = (0.5 * step_member) * (kappa + up_x(kappa))
        north = (0.5 * step_member) * (kappa + up_y(kappa))
        return east, north, step_member * spin

    def steps(p, q, east, north, spin):
        for _ in range(MSTEPS):
            moved = []
            for f in (p, q):
                fx = east * (up_x(f) - f)
                fy = north * (up_y(f) - f)
                moved.append(f + ((fx - low_x(fx)) + (fy - low_y(fy))))
            p, q = moved[0] - spin * q, moved[1] + spin * p
        return p[:rows, :cols], q[:rows, :cols]

    lane = lane_ids(EIGHT)
    pairs = range(2)

    def up_pair(own, side):
        ra, rb = pltpu.roll(own, LANES - 1, 1), pltpu.roll(side, LANES - 1, 1)
        return jnp.where(lane == LANES - 1, rb, ra), jnp.where(lane == LANES - 1, ra, rb)

    def low_pair(own, side):
        ra, rb = pltpu.roll(own, 1, 1), pltpu.roll(side, 1, 1)
        return jnp.where(lane == 0, rb, ra), jnp.where(lane == 0, ra, rb)

    def stage_group(lg):
        @pl.loop(0, EIGHT)
        def _(ls):
            l = lg * EIGHT + ls
            at = pl.ds(pl.multiple_of(ls * mheight, EIGHT), mheight)

            def put(g, value):
                stage[g, 0, at] = value[:, :cols]
                stage[g, 1, at] = value[:, cols:]

            for g in range(base):
                t = g * levels + l
                own = m_ref[g // fields, g % fields, l]
                put(g, extend(own, nm[t], prm[t], side_values(ym_in, mcor_in, g), l))
            t = base * levels + l
            put(base, extend(d_ref[l], nm[t], prm[t], side_values(ym_in, mcor_in, base), l))
            t = (base + 1) * levels
            spin = extend(r_ref[...], nm[t], prm[t], side_values(ym_in, mcor_in, base + 1), 0)
            put(base + 1, step_member * spin)

        @pl.loop(0, mheight, unroll=4)
        def _(i):
            src = lax.rem(i + mheight - H, mheight)
            for g in range(base + 2):
                for b in pairs:
                    rowwise[g, b, i] = stage[g, b, pl.ds(src, EIGHT, stride=mheight), :]

        @pl.loop(0, mheight - 1, unroll=4)
        def _(i):
            k = [rowwise[base, b, i] for b in pairs]
            up = up_pair(*k)
            for b in pairs:
                faces[0, b, i] = (0.5 * step_member) * (k[b] + rowwise[base, b, i + 1])
                faces[1, b, i] = (0.5 * step_member) * (k[b] + up[b])

    def run_group(lg):
        for step in range(MSTEPS):
            lo, hi = step + 1, mheight - 1 - step
            last = step == MSTEPS - 1
            now = [[rowwise[g, b, lo] for b in pairs] for g in range(base)]
            flux = [
                [faces[0, b, lo - 1] * (now[g][b] - rowwise[g, b, lo - 1]) for b in pairs]
                for g in range(base)
            ]

            def row(i, carry):
                now, flux = carry
                east = [faces[0, b, i] for b in pairs]
                north = [faces[1, b, i] for b in pairs]
                spin = [rowwise[base + 1, b, i] for b in pairs]
                after = [[rowwise[g, b, i + 1] for b in pairs] for g in range(base)]
                new_flux, moved = [], []
                for g in range(base):
                    f = now[g]
                    fx = [east[b] * (after[g][b] - f[b]) for b in pairs]
                    up = up_pair(*f)
                    fy = [north[b] * (up[b] - f[b]) for b in pairs]
                    low = low_pair(*fy)
                    moved.append(
                        [f[b] + ((fx[b] - flux[g][b]) + (fy[b] - low[b])) for b in pairs]
                    )
                    new_flux.append(fx)
                for g in range(0, base, 2):
                    for b in pairs:
                        p = moved[g][b] - spin[b] * now[g + 1][b]
                        q = moved[g + 1][b] + spin[b] * now[g][b]
                        if not last:
                            rowwise[g, b, i] = p
                            rowwise[g + 1, b, i] = q
                        elif b == 0:
                            for h, value in ((g, p), (g + 1, q)):
                                at = (h * levels + lg * EIGHT) * rows + i - H
                                mf_ref[pl.ds(at, EIGHT, stride=rows), :] = value
                return after, new_flux

            lax.fori_loop(lo, hi, row, (now, flux), unroll=2)

    def correction_level(l):
        w = weights(me * clevels + l)
        pair = []
        for f in range(fields):
            t = f * clevels + l
            pair.append(extend(corr[l, f], ncorr[t], prcorr[t], side_values(ycorr_in, kcor_in, f), l))
        shift[l, 0], shift[l, 1] = steps(*pair, *w)

    stage_group(0)
    landed(got_yk)
    got_kc = send_corners(ycorr_in, kcor, kcor_in)
    run_group(0)
    landed(got_xk)
    landed(got_kc)
    pl.loop(0, clevels)(correction_level)
    got_shift = [send(shift, shift_in.at[k], peers[k]) for k in range(n - 1)]
    for lg in range(1, levels // EIGHT):
        stage_group(lg)
        run_group(lg)

    def add(piece, owner):
        @pl.loop(0, clevels)
        def _(l):
            for f in range(fields):
                tile = piece[l, f]
                for m in range(count):
                    first = ((m * fields + f) * levels + owner * clevels + l) * rows
                    at = pl.ds(pl.multiple_of(first, EIGHT), rows)
                    mf_ref[at, :] = mf_ref[at, :] + tile

    add(shift, me)
    for k in range(n - 1):
        landed([got_shift[k]])
        add(shift_in.at[k], lax.rem(me + n - 1 - k, n))
    for copy in pending:
        copy.wait_send()
    assert len(pending) == copies


def per_device(control, members, diffusivity, rotation):
    fields, clevels, crows, ccols = control.shape
    count, _, levels, rows, cols = members.shape
    base = count * fields
    tiles = (base + 1) * levels + 1
    n = lax.axis_size("mem")
    ns = 2 if lax.axis_size("gy") > 2 else 1
    copies = 3 * (ns + 2 + 2 * ns) + 2 * (n - 1)
    vmem = lambda *shape: pltpu.VMEM(shape, F32)
    scratch = (
        [vmem(fields * clevels, H, ccols)] * 4
        + [vmem(tiles, H, cols)] * 4
        + [vmem(1, crows, LANES), vmem(base + 2, rows, LANES)]
        + [vmem(ns, 1, crows, LANES), vmem(ns, base + 2, rows, LANES)]
        + [vmem(ns, 2, 1, H, LANES), vmem(ns, 2, base + 2, H, LANES)] * 2
        + [vmem(levels, fields, rows, cols), vmem(n - 1, clevels, fields, rows, cols)]
        + [vmem(clevels, fields, rows, cols)]
        + [vmem(fields * clevels, H, cols)] * 4
        + [vmem(fields, rows, LANES), vmem(ns, fields, rows, LANES)]
        + [vmem(ns, 2, fields, H, LANES)] * 2
        + [vmem(clevels, fields, rows, cols), vmem(n - 1, clevels, fields, rows, cols)]
        + [vmem(base + 2, 2, EIGHT * (rows + 2 * H), LANES)]
        + [vmem(base + 2, 2, rows + 2 * H, EIGHT, LANES), vmem(2, 2, rows + 2 * H, EIGHT, LANES)]
        + [pltpu.SemaphoreType.DMA((copies,))] * 2
    )
    control_final, flat = pl.pallas_call(
        functools.partial(fused_kernel, copies),
        in_specs=[pl.BlockSpec(memory_space=pltpu.VMEM)] * 4,
        out_specs=[pl.BlockSpec(memory_space=pltpu.VMEM)] * 2,
        out_shape=[
            jax.ShapeDtypeStruct(control.shape, F32),
            jax.ShapeDtypeStruct((members.size // cols, cols), F32),
        ],
        scratch_shapes=scratch,
        compiler_params=pltpu.CompilerParams(collective_id=0, has_side_effects=True),
        name="fused",
    )(control, members, diffusivity, rotation)
    return control_final, flat.reshape(members.shape)


def solution(mesh):
    in_specs = (
        P(None, "mem", "gx", "gy"),
        P("mem", None, None, "gx", "gy"),
        P(None, "gx", "gy"),
        P("gx", "gy"),
    )
    out_specs = (P(None, "mem", "gx", "gy"), P("mem", None, None, "gx", "gy"))
    return jax.shard_map(
        per_device, mesh=mesh, in_specs=in_specs, out_specs=out_specs, check_vma=False
    )
```

```python
import functools

import jax
import jax.numpy as jnp
from jax import lax
from jax.experimental import pallas as pl
from jax.experimental.pallas import tpu as pltpu
from jax.sharding import PartitionSpec as P

CSTEPS = 4
MSTEPS = 4
H = 4
SLOT = 2 * H
LANES = 128
EIGHT = 8
CHUNK = 8

step_control = 0.15
viscosity = 0.5
step_member = 0.5
F32 = jnp.float32


def lane_ids(rows):
    return lax.broadcasted_iota(jnp.int32, (rows, LANES), 1)


def put_slot(packed, edges, slot):
    shift = H + SLOT * slot
    if not isinstance(slot, int):
        shift = lax.rem(shift, LANES)
    rolled = pltpu.roll(edges, shift, 1)
    ids = lane_ids(edges.shape[0])
    inside = (ids >= SLOT * slot) & (ids < SLOT * slot + SLOT)
    return jnp.where(inside, rolled, packed)


def side_block(left, right, slot):
    shift = lax.rem(2 * LANES - SLOT * slot - H, LANES)
    after = pltpu.roll(right, shift, 1)
    if left is right:
        return after
    before = pltpu.roll(left, shift, 1)
    return jnp.where(lane_ids(after.shape[0]) < LANES // 2, after, before)


def fused_kernel(
    copies, c_ref, m_ref, d_ref, r_ref, cf_ref, mf_ref,
    hc, tc, nc, prc, hm, tm, nm, prm, yc, ym, yc_in, ym_in, ccor, mcor, ccor_in, mcor_in,
    sums, sums_in, corr, hcorr, tcorr, ncorr, prcorr, ycorr, ycorr_in, kcor, kcor_in,
    shift, shift_in, stage, rowwise, faces, send_sem, recv_sem,
):
    fields, clevels, crows, ccols = c_ref.shape
    count, _, levels, rows, cols = m_ref.shape
    base = count * fields
    nx, ny, n = lax.axis_size("gx"), lax.axis_size("gy"), lax.axis_size("mem")
    x, y, me = lax.axis_index("gx"), lax.axis_index("gy"), lax.axis_index("mem")
    two = ny > 2
    nsides = 2 if two else 1
    x_next, x_prev = {"gx": lax.rem(x + 1, nx)}, {"gx": lax.rem(x + nx - 1, nx)}
    y_next, y_prev = {"gy": lax.rem(y + 1, ny)}, {"gy": lax.rem(y + ny - 1, ny)}
    peers = [{"mem": lax.rem(me + k, n)} for k in range(1, n)]
    mesh_id = pl.DeviceIdType.MESH
    pending = []

    def send(src, dst, target):
        k = len(pending)
        copy = pltpu.make_async_remote_copy(
            src_ref=src, dst_ref=dst, send_sem=send_sem.at[k], recv_sem=recv_sem.at[k],
            device_id=target, device_id_type=mesh_id,
        )
        copy.start()
        pending.append(copy)
        return copy

    def landed(group):
        for copy in group:
            copy.wait_recv()

    def send_y(src, dst):
        group = [send(src, dst.at[0], y_next)]
        if two:
            group.append(send(src, dst.at[1], y_prev))
        return group

    def send_x(first, last, from_next, from_prev):
        return [send(first, from_next, x_prev), send(last, from_prev, x_next)]

    def send_corners(got, buf, buf_in):
        group = []
        for side in range(nsides):
            for g in range(got.shape[1]):
                tile = got[side, g]
                buf[side, 0, g] = tile[:H]
                buf[side, 1, g] = tile[tile.shape[0] - H :]
            group += send_x(
                buf.at[side, 0], buf.at[side, 1], buf_in.at[side, 0], buf_in.at[side, 1]
            )
        return group

    barrier = pltpu.get_barrier_semaphore()
    greeted = [x_next, x_prev, y_next] + ([y_prev] if two else []) + peers
    for target in greeted:
        pl.semaphore_signal(barrier, inc=1, device_id=target, device_id_type=mesh_id)

    ids = lane_ids(crows)
    yc[...] = jnp.zeros_like(yc)
    ym[...] = jnp.zeros_like(ym)
    ycorr[...] = jnp.zeros_like(ycorr)

    @pl.loop(0, clevels)
    def _(l):
        for f in range(fields):
            first = c_ref[f, l, :, :LANES]
            last = c_ref[f, l, :, ccols - LANES :]
            t = f * clevels + l
            yc[0] = put_slot(yc[0], jnp.where(ids < LANES // 2, first, last), t)
            hc[t] = c_ref[f, l, :H]
            tc[t] = c_ref[f, l, crows - H :]

    pl.semaphore_wait(barrier, len(greeted))
    got_yc = send_y(yc, yc_in)
    got_xc = send_x(hc, tc, nc, prc)

    @pl.loop(0, levels)
    def _(l):
        for f in range(fields):
            total = None
            for m in range(count):
                tile = m_ref[m, f, l]
                total = tile if total is None else total + tile
                g = m * fields + f
                ym[g] = put_slot(ym[g], tile, l)
                hm[g * levels + l] = tile[:H]
                tm[g * levels + l] = tile[rows - H :]
            sums[l, f] = total
        tile = d_ref[l]
        ym[base] = put_slot(ym[base], tile, l)
        hm[base * levels + l] = tile[:H]
        tm[base * levels + l] = tile[rows - H :]

    tile = r_ref[...]
    ym[base + 1] = put_slot(jnp.zeros((rows, LANES), F32), tile, 0)
    hm[(base + 1) * levels] = tile[:H]
    tm[(base + 1) * levels] = tile[rows - H :]
    got_ym = send_y(ym, ym_in)
    got_xm = send_x(hm, tm, nm, prm)
    got_sum = []
    for k in range(1, n):
        owner = lax.rem(me + k, n)
        got_sum.append(send(sums.at[pl.ds(owner * clevels, clevels)], sums_in.at[k - 1], peers[k - 1]))

    landed(got_yc)
    got_cc = send_corners(yc_in, ccor, ccor_in)
    landed(got_xc)
    landed(got_cc)

    def side_values(body, corners, g):
        out = [
            jnp.concatenate([body[s, g], corners[s, 0, g], corners[s, 1, g]], axis=0)
            for s in range(nsides)
        ]
        return out[0], out[-1]

    half_x, half_y = crows // 2, ccols // 2
    height, full = crows + 2 * H, ccols + LANES

    def control_level(l):
        left, right = side_values(yc_in, ccor_in, 0)
        body = []
        for f in range(fields):
            t = f * clevels + l
            own = jnp.concatenate([c_ref[f, l], nc[t], prc[t]], axis=0)
            body.append(jnp.concatenate([own, side_block(left, right, t)], axis=1))
        for _ in range(CSTEPS):
            a = body[0] * (0.5 * step_control)
            b = body[1] * (0.5 * step_control)
            new = []
            for f in body:
                ux = pltpu.roll(f, height - 1, 0)
                lx = pltpu.roll(f, 1, 0)
                uy = pltpu.roll(f, full - 1, 1)
                ly = pltpu.roll(f, 1, 1)
                lap = (ux + lx) + (uy + ly) - 4.0 * f
                new.append(f + ((step_control * viscosity) * lap - a * (ux - lx) - b * (uy - ly)))
            body = new
        pick_y = (
            lax.broadcasted_iota(jnp.int32, (ccols, half_y), 0) // 2
            == lax.broadcasted_iota(jnp.int32, (ccols, half_y), 1)
        ).astype(F32)
        pick_x = (
            lax.broadcasted_iota(jnp.int32, (half_x, crows), 1) // 2
            == lax.broadcasted_iota(jnp.int32, (half_x, crows), 0)
        ).astype(F32)
        for f in range(fields):
            field = body[f][:crows, :ccols]
            cf_ref[f, l] = field
            t = jnp.dot(field, pick_y, precision=lax.Precision.HIGHEST, preferred_element_type=F32)
            t = jnp.dot(pick_x, t, precision=lax.Precision.HIGHEST, preferred_element_type=F32)
            corr[l, f] = 0.25 * t

    landed(got_ym)
    got_mc = send_corners(ym_in, mcor, mcor_in)
    pl.loop(0, clevels)(control_level)
    landed(got_sum)

    @pl.loop(0, clevels)
    def _(l):
        for f in range(fields):
            total = sums[me * clevels + l, f]
            for k in range(n - 1):
                total = total + sums_in[k, l, f]
            tile = corr[l, f] - total * (1.0 / (count * n))
            corr[l, f] = tile
            ycorr[f] = put_slot(ycorr[f], tile, l)
            hcorr[f * clevels + l] = tile[:H]
            tcorr[f * clevels + l] = tile[rows - H :]

    got_yk = send_y(ycorr, ycorr_in)
    got_xk = send_x(hcorr, tcorr, ncorr, prcorr)
    landed(got_xm)
    landed(got_mc)

    mheight, mfull = rows + 2 * H, cols + LANES
    up_x = lambda f: pltpu.roll(f, mheight - 1, 0)
    low_x = lambda f: pltpu.roll(f, 1, 0)
    up_y = lambda f: pltpu.roll(f, mfull - 1, 1)
    low_y = lambda f: pltpu.roll(f, 1, 1)

    def extend(own, after, before, sides, slot):
        own = jnp.concatenate([own, after, before], axis=0)
        return jnp.concatenate([own, side_block(*sides, slot)], axis=1)

    def weights(l):
        t = base * levels + l
        kappa = extend(d_ref[l], nm[t], prm[t], side_values(ym_in, mcor_in, base), l)
        t = (base + 1) * levels
        spin = extend(r_ref[...], nm[t], prm[t], side_values(ym_in, mcor_in, base + 1), 0)
        east = (0.5 * step_member) * (kappa + up_x(kappa))
        north = (0.5 * step_member) * (kappa + up_y(kappa))
        return east, north, step_member * spin

    def steps(p, q, east, north, spin):
        for _ in range(MSTEPS):
            moved = []
            for f in (p, q):
                fx = east * (up_x(f) - f)
                fy = north * (up_y(f) - f)
                moved.append(f + ((fx - low_x(fx)) + (fy - low_y(fy))))
            p, q = moved[0] - spin * q, moved[1] + spin * p
        return p[:rows, :cols], q[:rows, :cols]

    lane = lane_ids(EIGHT)
    pairs = range(2)

    def up_pair(own, side):
        ra, rb = pltpu.roll(own, LANES - 1, 1), pltpu.roll(side, LANES - 1, 1)
        return jnp.where(lane == LANES - 1, rb, ra), jnp.where(lane == LANES - 1, ra, rb)

    def low_pair(own, side):
        ra, rb = pltpu.roll(own, 1, 1), pltpu.roll(side, 1, 1)
        return jnp.where(lane == 0, rb, ra), jnp.where(lane == 0, ra, rb)

    for i in (mheight, mheight + 1):
        for b in pairs:
            for g in range(base + 2):
                rowwise[g, b, i] = jnp.zeros((EIGHT, LANES), F32)
            for g in range(2):
                faces[g, b, i] = jnp.zeros((EIGHT, LANES), F32)
                faces[g, b, mheight - 1] = jnp.zeros((EIGHT, LANES), F32)

    def stage_group(lg):
        @pl.loop(0, EIGHT)
        def _(ls):
            l = lg * EIGHT + ls
            at = pl.ds(pl.multiple_of(ls * mheight, EIGHT), mheight)

            def put(g, value):
                stage[g, 0, at] = value[:, :cols]
                stage[g, 1, at] = value[:, cols:]

            for g in range(base):
                t = g * levels + l
                own = m_ref[g // fields, g % fields, l]
                put(g, extend(own, nm[t], prm[t], side_values(ym_in, mcor_in, g), l))
            t = base * levels + l
            put(base, extend(d_ref[l], nm[t], prm[t], side_values(ym_in, mcor_in, base), l))
            t = (base + 1) * levels
            spin = extend(r_ref[...], nm[t], prm[t], side_values(ym_in, mcor_in, base + 1), 0)
            put(base + 1, step_member * spin)

        @pl.loop(0, mheight // CHUNK)
        def _(c):
            for g in range(base + 2):
                values = []
                for k in range(CHUNK):
                    src = lax.rem(c * CHUNK + k + mheight - H, mheight)
                    values += [stage[g, b, pl.ds(src, EIGHT, stride=mheight), :] for b in pairs]
                for k in range(CHUNK):
                    for b in pairs:
                        rowwise[g, b, c * CHUNK + k] = values[2 * k + b]

        @pl.loop(0, mheight // CHUNK)
        def _(c):
            i = c * CHUNK
            kappa = [[rowwise[base, b, i + k] for b in pairs] for k in range(CHUNK + 1)]
            ups = [up_pair(*kappa[k]) for k in range(CHUNK)]
            for k in range(CHUNK):
                for b in pairs:
                    faces[0, b, i + k] = (0.5 * step_member) * (kappa[k][b] + kappa[k + 1][b])
                    faces[1, b, i + k] = (0.5 * step_member) * (kappa[k][b] + ups[k][b])

    def run_group(lg):
        for g in range(0, base, 2):
            for step in range(MSTEPS):
                run_pair(lg, g, step == MSTEPS - 1)

    def run_pair(lg, g, last):
        lo = H if last else 1
        chunks = (rows if last else mheight) // CHUNK
        tiles = [(h, b) for h in (g, g + 1) for b in pairs]
        now = [rowwise[h, b, lo] for h, b in tiles]
        flux = [faces[0, b, lo - 1] * (rowwise[h, b, lo] - rowwise[h, b, lo - 1]) for h, b in tiles]

        def chunk(c, carry):
            now, flux = carry
            i = lo + c * CHUNK
            ks = range(CHUNK)
            f = [[now[t]] + [rowwise[h, b, i + 1 + k] for k in ks] for t, (h, b) in enumerate(tiles)]
            east = [[faces[0, b, i + k] for k in ks] for b in pairs]
            north = [[faces[1, b, i + k] for k in ks] for b in pairs]
            spin = [[rowwise[base + 1, b, i + k] for k in ks] for b in pairs]
            fx = [
                [flux[t]] + [east[b][k] * (f[t][k + 1] - f[t][k]) for k in ks]
                for t, (h, b) in enumerate(tiles)
            ]
            out = []
            for first in (0, 2):
                up = [up_pair(f[first][k], f[first + 1][k]) for k in ks]
                fy = [[north[b][k] * (up[k][b] - f[first + b][k]) for k in ks] for b in pairs]
                low = [low_pair(fy[0][k], fy[1][k]) for k in ks]
                for b in pairs:
                    t = first + b
                    out.append(
                        [
                            f[t][k] + ((fx[t][k + 1] - fx[t][k]) + (fy[b][k] - low[k][b]))
                            for k in ks
                        ]
                    )
            for b in pairs:
                if last and b == 1:
                    continue
                for k in ks:
                    p = out[b][k] - spin[b][k] * f[2 + b][k]
                    q = out[2 + b][k] + spin[b][k] * f[b][k]
                    for h, value in ((g, p), (g + 1, q)):
                        if last:
                            at = (h * levels + lg * EIGHT) * rows + c * CHUNK + k
                            mf_ref[pl.ds(at, EIGHT, stride=rows), :] = value
                        else:
                            rowwise[h, b, i + k] = value
            return [f[t][CHUNK] for t in range(4)], [fx[t][CHUNK] for t in range(4)]

        lax.fori_loop(0, chunks, chunk, (now, flux))

    def correction_level(l):
        w = weights(me * clevels + l)
        pair = []
        for f in range(fields):
            t = f * clevels + l
            pair.append(extend(corr[l, f], ncorr[t], prcorr[t], side_values(ycorr_in, kcor_in, f), l))
        shift[l, 0], shift[l, 1] = steps(*pair, *w)

    stage_group(0)
    landed(got_yk)
    got_kc = send_corners(ycorr_in, kcor, kcor_in)
    run_group(0)
    landed(got_xk)
    landed(got_kc)
    pl.loop(0, clevels)(correction_level)
    got_shift = [send(shift, shift_in.at[k], peers[k]) for k in range(n - 1)]
    for lg in range(1, levels // EIGHT):
        stage_group(lg)
        run_group(lg)

    def add(piece, owner):
        @pl.loop(0, clevels)
        def _(l):
            for f in range(fields):
                tile = piece[l, f]
                for m in range(count):
                    first = ((m * fields + f) * levels + owner * clevels + l) * rows
                    at = pl.ds(pl.multiple_of(first, EIGHT), rows)
                    mf_ref[at, :] = mf_ref[at, :] + tile

    add(shift, me)
    for k in range(n - 1):
        landed([got_shift[k]])
        add(shift_in.at[k], lax.rem(me + n - 1 - k, n))
    for copy in pending:
        copy.wait_send()
    assert len(pending) == copies


def per_device(control, members, diffusivity, rotation):
    fields, clevels, crows, ccols = control.shape
    count, _, levels, rows, cols = members.shape
    base = count * fields
    tiles = (base + 1) * levels + 1
    n = lax.axis_size("mem")
    ns = 2 if lax.axis_size("gy") > 2 else 1
    copies = 3 * (ns + 2 + 2 * ns) + 2 * (n - 1)
    vmem = lambda *shape: pltpu.VMEM(shape, F32)
    scratch = (
        [vmem(fields * clevels, H, ccols)] * 4
        + [vmem(tiles, H, cols)] * 4
        + [vmem(1, crows, LANES), vmem(base + 2, rows, LANES)]
        + [vmem(ns, 1, crows, LANES), vmem(ns, base + 2, rows, LANES)]
        + [vmem(ns, 2, 1, H, LANES), vmem(ns, 2, base + 2, H, LANES)] * 2
        + [vmem(levels, fields, rows, cols), vmem(n - 1, clevels, fields, rows, cols)]
        + [vmem(clevels, fields, rows, cols)]
        + [vmem(fields * clevels, H, cols)] * 4
        + [vmem(fields, rows, LANES), vmem(ns, fields, rows, LANES)]
        + [vmem(ns, 2, fields, H, LANES)] * 2
        + [vmem(clevels, fields, rows, cols), vmem(n - 1, clevels, fields, rows, cols)]
        + [vmem(base + 2, 2, EIGHT * (rows + 2 * H), LANES)]
        + [vmem(base + 2, 2, rows + 2 * H + 2, EIGHT, LANES), vmem(2, 2, rows + 2 * H + 2, EIGHT, LANES)]
        + [pltpu.SemaphoreType.DMA((copies,))] * 2
    )
    control_final, flat = pl.pallas_call(
        functools.partial(fused_kernel, copies),
        in_specs=[pl.BlockSpec(memory_space=pltpu.VMEM)] * 4,
        out_specs=[pl.BlockSpec(memory_space=pltpu.VMEM)] * 2,
        out_shape=[
            jax.ShapeDtypeStruct(control.shape, F32),
            jax.ShapeDtypeStruct((members.size // cols, cols), F32),
        ],
        scratch_shapes=scratch,
        compiler_params=pltpu.CompilerParams(collective_id=0, has_side_effects=True),
        name="fused",
    )(control, members, diffusivity, rotation)
    return control_final, flat.reshape(members.shape)


def solution(mesh):
    in_specs = (
        P(None, "mem", "gx", "gy"),
        P("mem", None, None, "gx", "gy"),
        P(None, "gx", "gy"),
        P("gx", "gy"),
    )
    out_specs = (P(None, "mem", "gx", "gy"), P("mem", None, None, "gx", "gy"))
    return jax.shard_map(
        per_device, mesh=mesh, in_specs=in_specs, out_specs=out_specs, check_vma=False
    )
```

```python
import functools

import jax
import jax.numpy as jnp
from jax import lax
from jax.experimental import pallas as pl
from jax.experimental.pallas import tpu as pltpu
from jax.sharding import PartitionSpec as P

CSTEPS = 4
MSTEPS = 4
H = 4
SLOT = 2 * H
LANES = 128

step_control = 0.15
viscosity = 0.5
step_member = 0.5
F32 = jnp.float32


def lane_ids(rows):
    return lax.broadcasted_iota(jnp.int32, (rows, LANES), 1)


def put_slot(packed, edges, slot):
    shift = H + SLOT * slot
    if not isinstance(slot, int):
        shift = lax.rem(shift, LANES)
    rolled = pltpu.roll(edges, shift, 1)
    ids = lane_ids(edges.shape[0])
    inside = (ids >= SLOT * slot) & (ids < SLOT * slot + SLOT)
    return jnp.where(inside, rolled, packed)


def side_block(left, right, slot):
    shift = lax.rem(2 * LANES - SLOT * slot - H, LANES)
    after = pltpu.roll(right, shift, 1)
    if left is right:
        return after
    before = pltpu.roll(left, shift, 1)
    return jnp.where(lane_ids(after.shape[0]) < LANES // 2, after, before)


def fused_kernel(
    copies, c_ref, m_ref, d_ref, r_ref, cf_ref, mf_ref,
    hc, tc, nc, prc, hm, tm, nm, prm, yc, ym, yc_in, ym_in, ccor, mcor, ccor_in, mcor_in,
    sums, sums_in, corr, hcorr, tcorr, ncorr, prcorr, ycorr, ycorr_in, kcor, kcor_in,
    shift, shift_in, send_sem, recv_sem,
):
    fields, clevels, crows, ccols = c_ref.shape
    count, _, levels, rows, cols = m_ref.shape
    base = count * fields
    nx, ny, n = lax.axis_size("gx"), lax.axis_size("gy"), lax.axis_size("mem")
    x, y, me = lax.axis_index("gx"), lax.axis_index("gy"), lax.axis_index("mem")
    two = ny > 2
    nsides = 2 if two else 1
    x_next, x_prev = {"gx": lax.rem(x + 1, nx)}, {"gx": lax.rem(x + nx - 1, nx)}
    y_next, y_prev = {"gy": lax.rem(y + 1, ny)}, {"gy": lax.rem(y + ny - 1, ny)}
    peers = [{"mem": lax.rem(me + k, n)} for k in range(1, n)]
    mesh_id = pl.DeviceIdType.MESH
    pending = []

    def send(src, dst, target):
        k = len(pending)
        copy = pltpu.make_async_remote_copy(
            src_ref=src, dst_ref=dst, send_sem=send_sem.at[k], recv_sem=recv_sem.at[k],
            device_id=target, device_id_type=mesh_id,
        )
        copy.start()
        pending.append(copy)
        return copy

    def landed(group):
        for copy in group:
            copy.wait_recv()

    def send_y(src, dst):
        group = [send(src, dst.at[0], y_next)]
        if two:
            group.append(send(src, dst.at[1], y_prev))
        return group

    def send_x(first, last, from_next, from_prev):
        return [send(first, from_next, x_prev), send(last, from_prev, x_next)]

    def send_corners(got, buf, buf_in):
        group = []
        for side in range(nsides):
            for g in range(got.shape[1]):
                tile = got[side, g]
                buf[side, 0, g] = tile[:H]
                buf[side, 1, g] = tile[tile.shape[0] - H :]
            group += send_x(
                buf.at[side, 0], buf.at[side, 1], buf_in.at[side, 0], buf_in.at[side, 1]
            )
        return group

    barrier = pltpu.get_barrier_semaphore()
    greeted = [x_next, x_prev, y_next] + ([y_prev] if two else []) + peers
    for target in greeted:
        pl.semaphore_signal(barrier, inc=1, device_id=target, device_id_type=mesh_id)

    ids = lane_ids(crows)
    yc[...] = jnp.zeros_like(yc)
    ym[...] = jnp.zeros_like(ym)
    ycorr[...] = jnp.zeros_like(ycorr)

    @pl.loop(0, clevels)
    def _(l):
        for f in range(fields):
            first = c_ref[f, l, :, :LANES]
            last = c_ref[f, l, :, ccols - LANES :]
            t = f * clevels + l
            yc[0] = put_slot(yc[0], jnp.where(ids < LANES // 2, first, last), t)
            hc[t] = c_ref[f, l, :H]
            tc[t] = c_ref[f, l, crows - H :]

    pl.semaphore_wait(barrier, len(greeted))
    got_yc = send_y(yc, yc_in)
    got_xc = send_x(hc, tc, nc, prc)

    @pl.loop(0, levels)
    def _(l):
        for f in range(fields):
            total = None
            for m in range(count):
                tile = m_ref[m, f, l]
                total = tile if total is None else total + tile
                g = m * fields + f
                ym[g] = put_slot(ym[g], tile, l)
                hm[g * levels + l] = tile[:H]
                tm[g * levels + l] = tile[rows - H :]
            sums[l, f] = total
        tile = d_ref[l]
        ym[base] = put_slot(ym[base], tile, l)
        hm[base * levels + l] = tile[:H]
        tm[base * levels + l] = tile[rows - H :]

    tile = r_ref[...]
    ym[base + 1] = put_slot(jnp.zeros((rows, LANES), F32), tile, 0)
    hm[(base + 1) * levels] = tile[:H]
    tm[(base + 1) * levels] = tile[rows - H :]
    got_ym = send_y(ym, ym_in)
    got_xm = send_x(hm, tm, nm, prm)
    got_sum = []
    for k in range(1, n):
        owner = lax.rem(me + k, n)
        got_sum.append(send(sums.at[pl.ds(owner * clevels, clevels)], sums_in.at[k - 1], peers[k - 1]))

    landed(got_yc)
    got_cc = send_corners(yc_in, ccor, ccor_in)
    landed(got_xc)
    landed(got_cc)

    def side_values(body, corners, g):
        out = [
            jnp.concatenate([body[s, g], corners[s, 0, g], corners[s, 1, g]], axis=0)
            for s in range(nsides)
        ]
        return out[0], out[-1]

    half_x, half_y = crows // 2, ccols // 2
    height, full = crows + 2 * H, ccols + LANES

    def control_level(l):
        left, right = side_values(yc_in, ccor_in, 0)
        body = []
        for f in range(fields):
            t = f * clevels + l
            own = jnp.concatenate([c_ref[f, l], nc[t], prc[t]], axis=0)
            body.append(jnp.concatenate([own, side_block(left, right, t)], axis=1))
        for _ in range(CSTEPS):
            a = body[0] * (0.5 * step_control)
            b = body[1] * (0.5 * step_control)
            new = []
            for f in body:
                ux = pltpu.roll(f, height - 1, 0)
                lx = pltpu.roll(f, 1, 0)
                uy = pltpu.roll(f, full - 1, 1)
                ly = pltpu.roll(f, 1, 1)
                lap = (ux + lx) + (uy + ly) - 4.0 * f
                new.append(f + ((step_control * viscosity) * lap - a * (ux - lx) - b * (uy - ly)))
            body = new
        pick_y = (
            lax.broadcasted_iota(jnp.int32, (ccols, half_y), 0) // 2
            == lax.broadcasted_iota(jnp.int32, (ccols, half_y), 1)
        ).astype(F32)
        pick_x = (
            lax.broadcasted_iota(jnp.int32, (half_x, crows), 1) // 2
            == lax.broadcasted_iota(jnp.int32, (half_x, crows), 0)
        ).astype(F32)
        for f in range(fields):
            field = body[f][:crows, :ccols]
            cf_ref[f, l] = field
            t = jnp.dot(field, pick_y, precision=lax.Precision.HIGHEST, preferred_element_type=F32)
            t = jnp.dot(pick_x, t, precision=lax.Precision.HIGHEST, preferred_element_type=F32)
            corr[l, f] = 0.25 * t

    pl.loop(0, 1)(control_level)
    landed(got_ym)
    got_mc = send_corners(ym_in, mcor, mcor_in)
    pl.loop(1, clevels)(control_level)
    landed(got_sum)

    @pl.loop(0, clevels)
    def _(l):
        for f in range(fields):
            total = sums[me * clevels + l, f]
            for k in range(n - 1):
                total = total + sums_in[k, l, f]
            tile = corr[l, f] - total * (1.0 / (count * n))
            corr[l, f] = tile
            ycorr[f] = put_slot(ycorr[f], tile, l)
            hcorr[f * clevels + l] = tile[:H]
            tcorr[f * clevels + l] = tile[rows - H :]

    got_yk = send_y(ycorr, ycorr_in)
    got_xk = send_x(hcorr, tcorr, ncorr, prcorr)
    landed(got_xm)
    landed(got_mc)

    mheight, mfull = rows + 2 * H, cols + LANES
    up_x = lambda f: pltpu.roll(f, mheight - 1, 0)
    low_x = lambda f: pltpu.roll(f, 1, 0)
    up_y = lambda f: pltpu.roll(f, mfull - 1, 1)
    low_y = lambda f: pltpu.roll(f, 1, 1)

    def extend(own, after, before, sides, slot):
        own = jnp.concatenate([own, after, before], axis=0)
        return jnp.concatenate([own, side_block(*sides, slot)], axis=1)

    def weights(l):
        t = base * levels + l
        kappa = extend(d_ref[l], nm[t], prm[t], side_values(ym_in, mcor_in, base), l)
        t = (base + 1) * levels
        spin = extend(r_ref[...], nm[t], prm[t], side_values(ym_in, mcor_in, base + 1), 0)
        east = (0.5 * step_member) * (kappa + up_x(kappa))
        north = (0.5 * step_member) * (kappa + up_y(kappa))
        return east, north, step_member * spin

    def steps(p, q, east, north, spin):
        for _ in range(MSTEPS):
            moved = []
            for f in (p, q):
                fx = east * (up_x(f) - f)
                fy = north * (up_y(f) - f)
                moved.append(f + ((fx - low_x(fx)) + (fy - low_y(fy))))
            p, q = moved[0] - spin * q, moved[1] + spin * p
        return p[:rows, :cols], q[:rows, :cols]

    def member_level(l):
        w = weights(l)
        for m in range(count):
            pair = []
            for f in range(fields):
                g = m * fields + f
                t = g * levels + l
                pair.append(extend(m_ref[m, f, l], nm[t], prm[t], side_values(ym_in, mcor_in, g), l))
            mf_ref[m, 0, l], mf_ref[m, 1, l] = steps(*pair, *w)

    def correction_level(l):
        w = weights(me * clevels + l)
        pair = []
        for f in range(fields):
            t = f * clevels + l
            pair.append(extend(corr[l, f], ncorr[t], prcorr[t], side_values(ycorr_in, kcor_in, f), l))
        shift[l, 0], shift[l, 1] = steps(*pair, *w)

    cut_a, cut_b = (3 * levels) // 16, (6 * levels) // 16
    pl.loop(0, cut_a)(member_level)
    landed(got_yk)
    got_kc = send_corners(ycorr_in, kcor, kcor_in)
    pl.loop(cut_a, cut_b)(member_level)
    landed(got_xk)
    landed(got_kc)
    pl.loop(0, clevels)(correction_level)
    got_shift = [send(shift, shift_in.at[k], peers[k]) for k in range(n - 1)]
    pl.loop(cut_b, levels)(member_level)

    def add(piece, owner):
        @pl.loop(0, clevels)
        def _(l):
            for f in range(fields):
                tile = piece[l, f]
                for m in range(count):
                    at = owner * clevels + l
                    mf_ref[m, f, at] = mf_ref[m, f, at] + tile

    add(shift, me)
    for k in range(n - 1):
        landed([got_shift[k]])
        add(shift_in.at[k], lax.rem(me + n - 1 - k, n))
    for copy in pending:
        copy.wait_send()
    assert len(pending) == copies


def per_device(control, members, diffusivity, rotation):
    fields, clevels, crows, ccols = control.shape
    count, _, levels, rows, cols = members.shape
    base = count * fields
    tiles = (base + 1) * levels + 1
    n = lax.axis_size("mem")
    ns = 2 if lax.axis_size("gy") > 2 else 1
    copies = 3 * (ns + 2 + 2 * ns) + 2 * (n - 1)
    vmem = lambda *shape: pltpu.VMEM(shape, F32)
    scratch = (
        [vmem(fields * clevels, H, ccols)] * 4
        + [vmem(tiles, H, cols)] * 4
        + [vmem(1, crows, LANES), vmem(base + 2, rows, LANES)]
        + [vmem(ns, 1, crows, LANES), vmem(ns, base + 2, rows, LANES)]
        + [vmem(ns, 2, 1, H, LANES), vmem(ns, 2, base + 2, H, LANES)] * 2
        + [vmem(levels, fields, rows, cols), vmem(n - 1, clevels, fields, rows, cols)]
        + [vmem(clevels, fields, rows, cols)]
        + [vmem(fields * clevels, H, cols)] * 4
        + [vmem(fields, rows, LANES), vmem(ns, fields, rows, LANES)]
        + [vmem(ns, 2, fields, H, LANES)] * 2
        + [vmem(clevels, fields, rows, cols), vmem(n - 1, clevels, fields, rows, cols)]
        + [pltpu.SemaphoreType.DMA((copies,))] * 2
    )
    return pl.pallas_call(
        functools.partial(fused_kernel, copies),
        in_specs=[pl.BlockSpec(memory_space=pltpu.VMEM)] * 4,
        out_specs=[pl.BlockSpec(memory_space=pltpu.VMEM)] * 2,
        out_shape=[
            jax.ShapeDtypeStruct(control.shape, F32),
            jax.ShapeDtypeStruct(members.shape, F32),
        ],
        scratch_shapes=scratch,
        compiler_params=pltpu.CompilerParams(collective_id=0, has_side_effects=True),
        name="fused",
    )(control, members, diffusivity, rotation)


def solution(mesh):
    in_specs = (
        P(None, "mem", "gx", "gy"),
        P("mem", None, None, "gx", "gy"),
        P(None, "gx", "gy"),
        P("gx", "gy"),
    )
    out_specs = (P(None, "mem", "gx", "gy"), P("mem", None, None, "gx", "gy"))
    return jax.shard_map(
        per_device, mesh=mesh, in_specs=in_specs, out_specs=out_specs, check_vma=False
    )
```
